32 devices in a mesh: tm: 16 (over z, y, x), atom: 2 (over core).
Axes of the slice: x: 2, y: 2, z: 4, core: 2. Of those that a mesh axis runs over, the one named last changes fastest.
Arguments:
- positions: int32 [3, 512, 512], P(None, 'tm', 'atom'), may hold values from 0 to 16383, as said below
- velocities: float32 [3, 512, 512], P(None, 'tm', 'atom'), may hold values from -6 to 6
- species: int32 [512], P('atom'), may hold values 0 or 1
- wave_vectors: int32 [3, 256], replicated, may hold values from -64 to 64
Outputs:
- isf: float32 [6, 256, 256], P(None, 'tm', 'atom')
The draws below stay inside these ranges and needn't reach their ends.
Inputs may be any that keep to these rules, and one draw needn't show every extreme that they name: `positions`: coordinates are fixed-point fractions of the periodic box in units of 1/16384.
All inputs are finite; a program needn't handle non-finite values. No bound on the sum of `species` on one device may be relied on, other than what follows from the above.
Results may differ from the reference program's by a relative error of at most 0.0003.
Values sent between devices are 32-bit elements; how exact they have to be, the bound alone decides.
A program may use at most 64 MiB of HBM per device.

```python
import math
import jax
import jax.numpy as jnp
from jax import lax

WAVES = 256
WAVE_MAX = 64
STEP_MAX = 8
ATOMS = 512
FRAMES = 512
LAGS = 256


def draw_positions(key, part):
    start_key = jax.random.fold_in(key, 11)
    step_key = jax.random.fold_in(key, 12)
    anchor = jax.random.randint(start_key, (3, 1, ATOMS), 0, 16384)
    moves = jax.random.randint(step_key, (3, FRAMES, ATOMS), 0 - STEP_MAX, STEP_MAX + 1)
    return jnp.remainder(anchor + jnp.cumsum(moves, axis=1), 16384).astype(jnp.int32)


def touch_ends(values, key, least, high):
    place = [jax.random.randint(jax.random.fold_in(key, axis), (), 0, length) for axis, length in enumerate(values.shape)]
    main_axis = values.shape.index(max(values.shape))
    beside = place[:main_axis] + [(place[main_axis] + 1) % values.shape[main_axis]] + place[main_axis + 1:]
    return values.at[tuple(place)].set(least).at[tuple(beside)].set(high)


def shard_levels(rng, shape, pieces, smallest, largest):
    gain = 1.0
    for position, shards_of in pieces:
        steps = jax.random.uniform(jax.random.fold_in(jax.random.fold_in(rng, 6), position), (shards_of,), jnp.float32, smallest / len(pieces), largest / len(pieces))
        gain = gain * jnp.repeat(jnp.exp(steps), shape[position] // shards_of).reshape((-1,) + (1,) * (len(shape) - 1 - position))
    return gain


def bell_draw(key, shape, width, bound, cuts=(), kind=jnp.bfloat16):
    values = jax.random.normal(key, shape, jnp.float32) * width
    if len(cuts) > 0:
        values = shard_levels(key, shape, cuts, -0.22, 0.18) * values
    return jnp.clip(values, min=-bound, max=bound).astype(kind)


def setup_inputs(seed: int = 0) -> dict:
    key_of = jax.random.split(jax.random.key(seed), 5)
    return {
        "positions": draw_positions(jax.random.fold_in(key_of[4], 71), 0),
        "velocities": bell_draw(key_of[1], (3, FRAMES, ATOMS), 1.0, 6.0, ((1, 16), (2, 2)), jnp.float32),
        "species": touch_ends((jax.random.randint(key_of[2], (ATOMS,), 0, 5) < 1).astype(jnp.int32), jax.random.fold_in(key_of[2], 1), 0, 1),
        "wave_vectors": touch_ends(jax.random.randint(key_of[3], (3, WAVES), 0 - WAVE_MAX, WAVE_MAX + 1), jax.random.fold_in(key_of[3], 1), 0 - WAVE_MAX, WAVE_MAX).astype(jnp.int32),
    }


highest = lax.Precision.HIGHEST


def frame_block(pos_block, vel_block, species_onehot, wave_vectors):
    summed = (pos_block[0][:, :, None] * wave_vectors[0] + pos_block[1][:, :, None] * wave_vectors[1]
              + pos_block[2][:, :, None] * wave_vectors[2])
    angle_unit = jnp.float32(2.0 * math.pi / 16384.0)
    phase = jnp.remainder(summed, 16384).astype(jnp.float32) * angle_unit
    kinds = jnp.concatenate([jnp.ones_like(vel_block[:1]), vel_block], 0)
    weights = kinds[:, None] * species_onehot[None, :, None, :]
    cos_part = jnp.einsum('qsba,bak->qsbk', weights, jnp.cos(phase), precision=highest)
    sin_part = jnp.einsum('qsba,bak->qsbk', weights, jnp.sin(phase), precision=highest)
    return jnp.stack([cos_part, sin_part])


def reference(positions, velocities, species, wave_vectors):
    block_size = 8
    block_count = FRAMES // block_size
    species_onehot = jnp.stack([1 - species, species]).astype(jnp.float32)
    pos_blocks = positions.reshape(3, block_count, block_size, ATOMS).transpose(1, 0, 2, 3)
    vel_blocks = velocities.reshape(3, block_count, block_size, ATOMS).transpose(1, 0, 2, 3)
    raw_modes = lax.map(lambda operands: frame_block(operands[0], operands[1], species_onehot, wave_vectors),
                        (pos_blocks, vel_blocks))
    raw_modes = raw_modes.transpose(1, 2, 3, 0, 4, 5).reshape(2, 4, 2, FRAMES, WAVES)
    wave_scaled = wave_vectors.astype(jnp.float32) / WAVE_MAX
    current = (wave_scaled[0] * raw_modes[:, 1] + wave_scaled[1] * raw_modes[:, 2]
               + wave_scaled[2] * raw_modes[:, 3])
    modes = jnp.stack([raw_modes[:, 0], current], 1)
    signals = jnp.moveaxis(modes, 3, 4)
    spectra = jnp.fft.rfft(signals, n=2 * FRAMES, axis=-1)
    spec_a = spectra[:, :, 0]
    spec_b = spectra[:, :, 1]
    cross = jnp.stack([spec_a * jnp.conj(spec_a), spec_a * jnp.conj(spec_b), spec_b * jnp.conj(spec_b)], 2).sum(0)
    corr = jnp.fft.irfft(cross, n=2 * FRAMES, axis=-1)[..., :LAGS]
    lag_index = jnp.arange(LAGS, dtype=jnp.int32)
    isf = corr / (jnp.float32(ATOMS) * (FRAMES - lag_index).astype(jnp.float32))
    return isf.reshape(6, WAVES, LAGS).astype(jnp.float32)
```

```python
import math

import jax
import jax.numpy as jnp
import ml_dtypes
import numpy as np
from jax import lax
from jax.experimental import pallas as pl
from jax.experimental.pallas import tpu as pltpu
from jax.sharding import PartitionSpec as P

WAVE_MAX = 64


highest = lax.Precision.HIGHEST


def frame_block(pos_block, vel_block, species_onehot, wave_vectors):
    summed = (
        pos_block[0][:, :, None] * wave_vectors[0]
        + pos_block[1][:, :, None] * wave_vectors[1]
        + pos_block[2][:, :, None] * wave_vectors[2]
    )
    angle_unit = jnp.float32(2.0 * math.pi / 16384.0)
    phase = jnp.remainder(summed, 16384).astype(jnp.float32) * angle_unit
    kinds = jnp.concatenate([jnp.ones_like(vel_block[:1]), vel_block], 0)
    weights = kinds[:, None] * species_onehot[None, :, None, :]
    cos_part = jnp.einsum("qsba,bak->qsbk", weights, jnp.cos(phase), precision=highest)
    sin_part = jnp.einsum("qsba,bak->qsbk", weights, jnp.sin(phase), precision=highest)
    return jnp.stack([cos_part, sin_part])


def pair_terms(cos_rows, sin_rows):
    cos_a = cos_rows[:, :, 0]
    cos_b = cos_rows[:, :, 1]
    sin_a = sin_rows[:, :, 0]
    sin_b = sin_rows[:, :, 1]
    real_part = jnp.stack(
        [
            cos_a * cos_a + sin_a * sin_a,
            cos_a * cos_b + sin_a * sin_b,
            cos_b * cos_b + sin_b * sin_b,
        ],
        2,
    ).sum(0)
    imag_part = jnp.stack(
        [
            cos_a * sin_a - sin_a * cos_a,
            cos_a * sin_b - sin_a * cos_b,
            cos_b * sin_b - sin_b * cos_b,
        ],
        2,
    ).sum(0)
    return (real_part, imag_part)


def correlate(signals, atom_total):
    frame_total = signals.shape[-1]
    waves_here = signals.shape[3]
    signal_rows = signals.reshape(-1, frame_total)
    groups = lax.axis_size("atom")
    freq_count = frame_total // groups
    lag_count = frame_total // 2 // groups
    my_index = lax.axis_index("atom")
    freq_index = my_index * freq_count + jnp.arange(freq_count, dtype=jnp.int32)
    time_index = jnp.arange(frame_total, dtype=jnp.int32)
    angle_step = jnp.float32(math.pi / frame_total)
    turns = jnp.remainder(time_index[:, None] * freq_index[None, :], 2 * frame_total)
    angles = turns.astype(jnp.float32) * angle_step
    spec_cos = jnp.dot(signal_rows, jnp.cos(angles), precision=highest).reshape(
        2, 2, 2, waves_here, freq_count
    )
    spec_sin = jnp.dot(signal_rows, jnp.sin(angles), precision=highest).reshape(
        2, 2, 2, waves_here, freq_count
    )
    real_part, imag_part = pair_terms(spec_cos, spec_sin)
    spectral_weight = jnp.where(freq_index == 0, 1.0, 2.0).astype(jnp.float32)
    real_rows = (real_part * spectral_weight).reshape(6 * waves_here, freq_count)
    imag_rows = (imag_part * spectral_weight).reshape(6 * waves_here, freq_count)
    alternating = jnp.where(time_index % 2 == 0, 1.0, -1.0).astype(jnp.float32)
    nyquist = jnp.dot(signal_rows, alternating, precision=highest).reshape(2, 2, 2, waves_here)
    nyq_a = nyquist[:, :, 0]
    nyq_b = nyquist[:, :, 1]
    nyq_real = (
        jnp.stack([nyq_a * nyq_a, nyq_a * nyq_b, nyq_b * nyq_b], 2).sum(0).reshape(6 * waves_here)
    )
    nyq_here = nyq_real * jnp.where(my_index == 0, 1.0, 0.0).astype(jnp.float32)
    lag_index = jnp.arange(lag_count * lax.axis_size("atom"), dtype=jnp.int32)
    lag_turns = jnp.remainder(lag_index[:, None] * freq_index[None, :], 2 * frame_total)
    lag_angles = lag_turns.astype(jnp.float32) * angle_step
    term = jnp.dot(jnp.cos(lag_angles), real_rows.T, precision=highest) - jnp.dot(
        jnp.sin(lag_angles), imag_rows.T, precision=highest
    )
    lag_sign = jnp.where(lag_index % 2 == 0, 1.0, -1.0).astype(jnp.float32)
    shared = lax.psum_scatter(
        term + lag_sign[:, None] * nyq_here[None, :], "atom", scatter_dimension=0, tiled=True
    )
    lag_index = my_index * lag_count + jnp.arange(lag_count, dtype=jnp.int32)
    scaled = shared / jnp.float32(2 * frame_total)
    isf = (
        scaled / (jnp.float32(atom_total) * (frame_total - lag_index).astype(jnp.float32))[:, None]
    )
    return isf.T.reshape(6, waves_here, lag_count)


def per_device_general(positions, velocities, species, wave_vectors):
    atom_count = positions.shape[2]
    frame_count = positions.shape[1]
    wave_count = wave_vectors.shape[1]
    block_size = math.gcd(frame_count, 2)
    block_count = frame_count // block_size
    species_onehot = jnp.stack([1 - species, species]).astype(jnp.float32)
    pos_blocks = positions.reshape(3, block_count, block_size, atom_count).transpose(1, 0, 2, 3)
    vel_blocks = velocities.reshape(3, block_count, block_size, atom_count).transpose(1, 0, 2, 3)
    raw_modes = lax.map(
        lambda operands: frame_block(operands[0], operands[1], species_onehot, wave_vectors),
        (pos_blocks, vel_blocks),
    )
    raw_modes = raw_modes.transpose(1, 2, 3, 0, 4, 5).reshape(2, 4, 2, frame_count, wave_count)
    wave_scaled = wave_vectors.astype(jnp.float32) / WAVE_MAX
    current = (
        wave_scaled[0] * raw_modes[:, 1]
        + wave_scaled[1] * raw_modes[:, 2]
        + wave_scaled[2] * raw_modes[:, 3]
    )
    modes = jnp.stack([raw_modes[:, 0], current], 1)
    atom_groups = lax.axis_size("atom")
    summed = lax.psum(modes, "atom")
    owned = lax.all_to_all(summed, "tm", split_axis=4, concat_axis=3, tiled=True)
    signals = jnp.moveaxis(owned, 3, 4)
    return correlate(signals, atom_count * atom_groups)


GROUP = 16
STEP = 2


def even_coeffs(func, degree):
    fit = np.polynomial.chebyshev.Chebyshev.interpolate(
        lambda z: func(np.sqrt(np.maximum(z, 1e-12))), degree, domain=[0.0, 0.25]
    )
    return [float(v) for v in fit.convert(kind=np.polynomial.Polynomial).coef]


COS_COEFFS = even_coeffs(lambda r: np.cos(2 * np.pi * r), 5)
SIN_COEFFS = even_coeffs(lambda r: np.sin(2 * np.pi * r) / r, 4)


def dft_tables(frames):
    turns = np.outer(np.arange(frames), np.arange(frames)) % (2 * frames)
    angle = turns * (np.pi / frames)
    sine = np.sin(angle)
    sine[:, 0] = 1.0 - 2.0 * (np.arange(frames) % 2)
    table = np.concatenate([np.cos(angle), sine], 1).astype(np.float32)
    high = table.astype(ml_dtypes.bfloat16)
    low = (table - high.astype(np.float32)).astype(ml_dtypes.bfloat16)
    return np.stack([high, low])


def horner(coeffs, z):
    value = coeffs[-1] * z + coeffs[-2]
    for coeff in coeffs[-3::-1]:
        value = value * z + coeff
    return value


def split(value):
    high = value.astype(jnp.bfloat16)
    low = (value - high.astype(jnp.float32)).astype(jnp.bfloat16)
    return high, low


def dot_rows(left, right):
    return lax.dot_general(
        left, right, (((1,), (1,)), ((), ())), preferred_element_type=jnp.float32
    )


def fused_kernel(
    tm_size,
    pos_ref,
    vel_ref,
    species_ref,
    wave_ref,
    table_hbm,
    out_ref,
    table,
    wave_cols,
    factor,
    weights,
    acc,
    modes,
    from_pair,
    summed,
    signals,
    result,
    result_in,
    table_sem,
    pair_send,
    pair_recv,
    peer_send,
    peer_recv,
    last_send,
    last_recv,
):
    me = lax.axis_index("tm")
    core = lax.axis_index("atom")
    other = 1 - core
    frames = pos_ref.shape[1]
    waves = wave_ref.shape[1]
    atoms = pos_ref.shape[2]
    groups = frames // GROUP
    frame_total = frames * tm_size

    barrier = pltpu.get_barrier_semaphore()
    for hop in range(1, tm_size):
        peer = lax.rem(me + hop, tm_size)
        pl.semaphore_signal(
            barrier, inc=1, device_id=(peer, core), device_id_type=pl.DeviceIdType.MESH
        )
    pl.semaphore_signal(
        barrier, inc=1, device_id=(me, other), device_id_type=pl.DeviceIdType.MESH
    )
    table_copy = pltpu.make_async_copy(table_hbm, table, table_sem)
    table_copy.start()

    lane = lax.broadcasted_iota(jnp.int32, (waves, 128), 1)
    for d in range(3):
        row = wave_ref[d : d + 1, :].astype(jnp.float32)
        wave_cols[d] = jnp.broadcast_to(row, (128, waves)).T
    scaled = jnp.where(
        lane < 64, wave_cols[0], jnp.where(lane < 96, wave_cols[1], wave_cols[2])
    ) * (1.0 / WAVE_MAX)
    factor[...] = jnp.where(lane < 32, 1.0, scaled)
    species_b = species_ref[...].astype(jnp.float32)
    species_a = 1.0 - species_b

    def trig(t):
        turn = None
        for d in range(3):
            coord = pos_ref[d, pl.ds(t, 1), :].astype(jnp.float32) * (1.0 / 16384.0)
            wave = wave_cols[d]
            term = jnp.concatenate([wave] * (atoms // 128), 1) * coord
            turn = term if turn is None else turn + term
        magic = jnp.float32(12582912.0)
        rest = turn - ((turn + magic) - magic)
        z = rest * rest
        return horner(COS_COEFFS, z), rest * horner(SIN_COEFFS, z)

    def pair_copy(tg):
        return pltpu.make_async_remote_copy(
            src_ref=modes.at[tg, other],
            dst_ref=from_pair.at[tg],
            send_sem=pair_send.at[tg],
            recv_sem=pair_recv.at[tg],
            device_id=(me, other),
            device_id_type=pl.DeviceIdType.MESH,
        )

    def peer_copy(tg, hop):
        peer = lax.rem(me + hop, tm_size)
        return pltpu.make_async_remote_copy(
            src_ref=summed.at[tg, peer],
            dst_ref=signals.at[me, tg],
            send_sem=peer_send.at[tg, hop],
            recv_sem=peer_recv.at[tg, hop],
            device_id=(peer, core),
            device_id_type=pl.DeviceIdType.MESH,
        )

    def reduce_and_send(tg):
        pair_copy(tg).wait_recv()
        summed[tg] = modes[tg, core] + from_pair[tg]
        for hop in range(1, tm_size):
            peer_copy(tg, hop).start()
        signals[me, tg] = summed[tg, me]

    row_index = lax.broadcasted_iota(jnp.int32, (256, atoms), 0)
    for tg in range(groups):
        rows = []
        for q in range(4):
            for spec in (species_a, species_b):
                if q == 0:
                    rows.append(jnp.broadcast_to(spec, (GROUP, atoms)))
                else:
                    rows.append(vel_ref[q - 1, tg * GROUP : (tg + 1) * GROUP, :] * spec)
        kinds = jnp.concatenate(rows, 0)
        high, low = split(kinds)
        weights[0:128] = high.astype(jnp.float32)
        weights[128:256] = low.astype(jnp.float32)
        acc[...] = jnp.zeros_like(acc)

        def step(index, carry):
            left_cos, left_sin, right = [], [], []
            for k in range(STEP):
                local = index * STEP + k
                cosine, sine = trig(tg * GROUP + local)
                left_cos += list(split(cosine))
                left_sin += list(split(sine))
                frame_w = jnp.where(
                    (row_index & (GROUP - 1)) == local, weights[...], 0.0
                ).astype(jnp.bfloat16)
                right += [frame_w, frame_w]
            right = jnp.concatenate(right, 1)
            acc[0:waves] += dot_rows(jnp.concatenate(left_cos, 1), right)
            acc[waves : 2 * waves] += dot_rows(jnp.concatenate(left_sin, 1), right)
            return carry

        lax.fori_loop(0, GROUP // STEP, step, 0)
        halves = []
        for c in range(2):
            block = acc[c * waves : (c + 1) * waves]
            part = (block[:, :128] + block[:, 128:]) * factor[...]
            current = part + pltpu.roll(part, 96, 1) + pltpu.roll(part, 64, 1)
            halves.append(jnp.where(lane < 32, part, current))
        packed = jnp.where(lane < 64, halves[0], pltpu.roll(halves[1], 64, 1))
        packed = packed.reshape(tm_size, 2, 8, 128)
        modes[tg, 0] = packed[:, 0]
        modes[tg, 1] = packed[:, 1]
        if tg == 0:
            pl.semaphore_wait(barrier, tm_size)
        pair_copy(tg).start()
        reduce_and_send(tg)
    table_copy.wait()
    for tg in range(groups):
        for hop in range(1, tm_size):
            peer_copy(tg, hop).wait_recv()

    tiles = signals[...].reshape(frame_total // 128, 8, 8, 128)
    wide = frame_total // 128 * 8
    group_lane = lax.broadcasted_iota(jnp.int32, (wide, 128), 1) // 16
    turned = [
        pltpu.roll(tiles[:, p].reshape(wide, 128), 16 * p, 1) if p else tiles[:, p].reshape(wide, 128)
        for p in range(8)
    ]
    rows = []
    for m in range(8):
        picked = turned[0]
        for p in range(1, 8):
            picked = jnp.where(group_lane == (m + p) % 8, turned[p], picked)
        if m:
            picked = pltpu.roll(picked, 128 - 16 * m, 1)
        rows.append(
            jnp.concatenate([picked[v * 8 : v * 8 + 8] for v in range(frame_total // 128)], 1)
        )
    high, low = split(jnp.concatenate(rows, 0))
    both = jnp.dot(
        jnp.concatenate([high, low], 0), table[0], preferred_element_type=jnp.float32
    )
    spectra = both[:64] + both[64:] + jnp.dot(high, table[1], preferred_element_type=jnp.float32)
    first = lax.broadcasted_iota(jnp.int32, (8, frame_total), 1) == 0
    out_rows = []
    for g in range(2):
        for a, b in ((0, 0), (0, 1), (1, 1)):
            even = jnp.zeros((8, frame_total), jnp.float32)
            odd = jnp.zeros((8, frame_total), jnp.float32)
            imag = jnp.zeros((8, frame_total), jnp.float32)
            for c in range(2):
                row_a = (c * 4 + g * 2 + a) * 8
                row_b = (c * 4 + g * 2 + b) * 8
                cos_a = spectra[row_a : row_a + 8, :frame_total]
                sin_a = spectra[row_a : row_a + 8, frame_total:]
                cos_b = spectra[row_b : row_b + 8, :frame_total]
                sin_b = spectra[row_b : row_b + 8, frame_total:]
                even += cos_a * cos_b
                odd += sin_a * sin_b
                imag += sin_a * cos_b - cos_a * sin_b
            real = jnp.where(first, even, 2.0 * (even + odd))
            imag = jnp.where(first, odd, 2.0 * imag)
            out_rows.append(jnp.concatenate([real, imag], 1))
    high, low = split(jnp.concatenate(out_rows, 0))
    lags = 2 * out_ref.shape[2]
    both = dot_rows(jnp.concatenate([high, low], 0), table[0, :lags])
    corr = both[:48] + both[48:] + dot_rows(high, table[1, :lags])
    lag = lax.broadcasted_iota(jnp.int32, (1, lags), 1)
    norm = 1.0 / (
        (frame_total - lag).astype(jnp.float32) * jnp.float32(2 * frame_total * 2 * atoms)
    )
    corr = (corr * norm).reshape(6, 8, lags)
    result[0] = corr[:, :, : lags // 2]
    result[1] = corr[:, :, lags // 2 :]
    swap = pltpu.make_async_remote_copy(
        src_ref=result.at[other],
        dst_ref=result_in,
        send_sem=last_send,
        recv_sem=last_recv,
        device_id=(me, other),
        device_id_type=pl.DeviceIdType.MESH,
    )
    swap.start()
    out_ref[:, pl.ds(pl.multiple_of(core * 8, 8), 8), :] = result[core]
    for tg in range(groups):
        pair_copy(tg).wait_send()
        for hop in range(1, tm_size):
            peer_copy(tg, hop).wait_send()
    swap.wait()
    out_ref[:, pl.ds(pl.multiple_of(other * 8, 8), 8), :] = result_in[...]


def per_device_fused(tm_size, positions, velocities, species, wave_vectors):
    frames, atoms = positions.shape[1:]
    waves = wave_vectors.shape[1]
    groups = frames // GROUP
    frame_total = frames * tm_size
    lag_here = frame_total // 4
    vmem = pl.BlockSpec(memory_space=pltpu.VMEM)
    dma = pltpu.SemaphoreType.DMA
    return pl.pallas_call(
        lambda *refs: fused_kernel(tm_size, *refs),
        name="scattering",
        out_shape=jax.ShapeDtypeStruct((6, 16, lag_here), jnp.float32),
        in_specs=[vmem] * 4 + [pl.BlockSpec(memory_space=pl.ANY)],
        out_specs=vmem,
        scratch_shapes=[
            pltpu.VMEM((2, frame_total, 2 * frame_total), jnp.bfloat16),
            pltpu.VMEM((3, waves, 128), jnp.float32),
            pltpu.VMEM((waves, 128), jnp.float32),
            pltpu.VMEM((256, atoms), jnp.float32),
            pltpu.VMEM((2 * waves, 256), jnp.float32),
            pltpu.VMEM((groups, 2, tm_size, 8, 128), jnp.float32),
            pltpu.VMEM((groups, tm_size, 8, 128), jnp.float32),
            pltpu.VMEM((groups, tm_size, 8, 128), jnp.float32),
            pltpu.VMEM((tm_size, groups, 8, 128), jnp.float32),
            pltpu.VMEM((2, 6, 8, lag_here), jnp.float32),
            pltpu.VMEM((6, 8, lag_here), jnp.float32),
            dma,
            dma((groups,)),
            dma((groups,)),
            dma((groups, tm_size)),
            dma((groups, tm_size)),
            dma,
            dma,
        ],
        compiler_params=pltpu.CompilerParams(
            collective_id=0, has_side_effects=True, vmem_limit_bytes=48 << 20
        ),
    )(
        positions,
        velocities,
        species.reshape(1, atoms),
        wave_vectors,
        jnp.asarray(dft_tables(frame_total)),
    )


def solution(mesh):
    tm_size = mesh.shape["tm"]
    atom_size = mesh.shape["atom"]

    def per_device(positions, velocities, species, wave_vectors):
        frames, atoms = positions.shape[1:]
        waves = wave_vectors.shape[1]
        fits = (
            tm_size == 16
            and atom_size == 2
            and frames == 2 * GROUP
            and atoms == 256
            and waves == 256
        )
        if fits:
            return per_device_fused(tm_size, positions, velocities, species, wave_vectors)
        return per_device_general(positions, velocities, species, wave_vectors)

    return jax.shard_map(
        per_device,
        mesh=mesh,
        in_specs=(P(None, "tm", "atom"), P(None, "tm", "atom"), P("atom"), P()),
        out_specs=P(None, "tm", "atom"),
        check_vma=False,
    )
```

```python
import math

import jax
import jax.numpy as jnp
import ml_dtypes
import numpy as np
from jax import lax
from jax.experimental import pallas as pl
from jax.experimental.pallas import tpu as pltpu
from jax.sharding import PartitionSpec as P

WAVE_MAX = 64


highest = lax.Precision.HIGHEST


def frame_block(pos_block, vel_block, species_onehot, wave_vectors):
    summed = (
        pos_block[0][:, :, None] * wave_vectors[0]
        + pos_block[1][:, :, None] * wave_vectors[1]
        + pos_block[2][:, :, None] * wave_vectors[2]
    )
    angle_unit = jnp.float32(2.0 * math.pi / 16384.0)
    phase = jnp.remainder(summed, 16384).astype(jnp.float32) * angle_unit
    kinds = jnp.concatenate([jnp.ones_like(vel_block[:1]), vel_block], 0)
    weights = kinds[:, None] * species_onehot[None, :, None, :]
    cos_part = jnp.einsum("qsba,bak->qsbk", weights, jnp.cos(phase), precision=highest)
    sin_part = jnp.einsum("qsba,bak->qsbk", weights, jnp.sin(phase), precision=highest)
    return jnp.stack([cos_part, sin_part])


def pair_terms(cos_rows, sin_rows):
    cos_a = cos_rows[:, :, 0]
    cos_b = cos_rows[:, :, 1]
    sin_a = sin_rows[:, :, 0]
    sin_b = sin_rows[:, :, 1]
    real_part = jnp.stack(
        [
            cos_a * cos_a + sin_a * sin_a,
            cos_a * cos_b + sin_a * sin_b,
            cos_b * cos_b + sin_b * sin_b,
        ],
        2,
    ).sum(0)
    imag_part = jnp.stack(
        [
            cos_a * sin_a - sin_a * cos_a,
            cos_a * sin_b - sin_a * cos_b,
            cos_b * sin_b - sin_b * cos_b,
        ],
        2,
    ).sum(0)
    return (real_part, imag_part)


def correlate(signals, atom_total):
    frame_total = signals.shape[-1]
    waves_here = signals.shape[3]
    signal_rows = signals.reshape(-1, frame_total)
    groups = lax.axis_size("atom")
    freq_count = frame_total // groups
    lag_count = frame_total // 2 // groups
    my_index = lax.axis_index("atom")
    freq_index = my_index * freq_count + jnp.arange(freq_count, dtype=jnp.int32)
    time_index = jnp.arange(frame_total, dtype=jnp.int32)
    angle_step = jnp.float32(math.pi / frame_total)
    turns = jnp.remainder(time_index[:, None] * freq_index[None, :], 2 * frame_total)
    angles = turns.astype(jnp.float32) * angle_step
    spec_cos = jnp.dot(signal_rows, jnp.cos(angles), precision=highest).reshape(
        2, 2, 2, waves_here, freq_count
    )
    spec_sin = jnp.dot(signal_rows, jnp.sin(angles), precision=highest).reshape(
        2, 2, 2, waves_here, freq_count
    )
    real_part, imag_part = pair_terms(spec_cos, spec_sin)
    spectral_weight = jnp.where(freq_index == 0, 1.0, 2.0).astype(jnp.float32)
    real_rows = (real_part * spectral_weight).reshape(6 * waves_here, freq_count)
    imag_rows = (imag_part * spectral_weight).reshape(6 * waves_here, freq_count)
    alternating = jnp.where(time_index % 2 == 0, 1.0, -1.0).astype(jnp.float32)
    nyquist = jnp.dot(signal_rows, alternating, precision=highest).reshape(2, 2, 2, waves_here)
    nyq_a = nyquist[:, :, 0]
    nyq_b = nyquist[:, :, 1]
    nyq_real = (
        jnp.stack([nyq_a * nyq_a, nyq_a * nyq_b, nyq_b * nyq_b], 2).sum(0).reshape(6 * waves_here)
    )
    nyq_here = nyq_real * jnp.where(my_index == 0, 1.0, 0.0).astype(jnp.float32)
    lag_index = jnp.arange(lag_count * lax.axis_size("atom"), dtype=jnp.int32)
    lag_turns = jnp.remainder(lag_index[:, None] * freq_index[None, :], 2 * frame_total)
    lag_angles = lag_turns.astype(jnp.float32) * angle_step
    term = jnp.dot(jnp.cos(lag_angles), real_rows.T, precision=highest) - jnp.dot(
        jnp.sin(lag_angles), imag_rows.T, precision=highest
    )
    lag_sign = jnp.where(lag_index % 2 == 0, 1.0, -1.0).astype(jnp.float32)
    shared = lax.psum_scatter(
        term + lag_sign[:, None] * nyq_here[None, :], "atom", scatter_dimension=0, tiled=True
    )
    lag_index = my_index * lag_count + jnp.arange(lag_count, dtype=jnp.int32)
    scaled = shared / jnp.float32(2 * frame_total)
    isf = (
        scaled / (jnp.float32(atom_total) * (frame_total - lag_index).astype(jnp.float32))[:, None]
    )
    return isf.T.reshape(6, waves_here, lag_count)


def per_device_general(positions, velocities, species, wave_vectors):
    atom_count = positions.shape[2]
    frame_count = positions.shape[1]
    wave_count = wave_vectors.shape[1]
    block_size = math.gcd(frame_count, 2)
    block_count = frame_count // block_size
    species_onehot = jnp.stack([1 - species, species]).astype(jnp.float32)
    pos_blocks = positions.reshape(3, block_count, block_size, atom_count).transpose(1, 0, 2, 3)
    vel_blocks = velocities.reshape(3, block_count, block_size, atom_count).transpose(1, 0, 2, 3)
    raw_modes = lax.map(
        lambda operands: frame_block(operands[0], operands[1], species_onehot, wave_vectors),
        (pos_blocks, vel_blocks),
    )
    raw_modes = raw_modes.transpose(1, 2, 3, 0, 4, 5).reshape(2, 4, 2, frame_count, wave_count)
    wave_scaled = wave_vectors.astype(jnp.float32) / WAVE_MAX
    current = (
        wave_scaled[0] * raw_modes[:, 1]
        + wave_scaled[1] * raw_modes[:, 2]
        + wave_scaled[2] * raw_modes[:, 3]
    )
    modes = jnp.stack([raw_modes[:, 0], current], 1)
    atom_groups = lax.axis_size("atom")
    summed = lax.psum(modes, "atom")
    owned = lax.all_to_all(summed, "tm", split_axis=4, concat_axis=3, tiled=True)
    signals = jnp.moveaxis(owned, 3, 4)
    return correlate(signals, atom_count * atom_groups)


GROUP = 16
STEP = 4


def even_coeffs(func, degree):
    fit = np.polynomial.chebyshev.Chebyshev.interpolate(
        lambda z: func(np.sqrt(np.maximum(z, 1e-12))), degree, domain=[0.0, 0.25]
    )
    return [float(v) for v in fit.convert(kind=np.polynomial.Polynomial).coef]


COS_COEFFS = even_coeffs(lambda r: np.sqrt(2.0) * np.cos(np.pi * r), 3)
SIN_COEFFS = even_coeffs(lambda r: np.sqrt(2.0) * np.sin(np.pi * r) / r, 3)


def dft_tables(frames):
    turns = np.outer(np.arange(frames), np.arange(frames)) % (2 * frames)
    angle = turns * (np.pi / frames)
    sine = np.sin(angle)
    sine[:, 0] = 1.0 - 2.0 * (np.arange(frames) % 2)
    table = np.concatenate([np.cos(angle), sine], 1).astype(np.float32)
    high = table.astype(ml_dtypes.bfloat16)
    low = (table - high.astype(np.float32)).astype(ml_dtypes.bfloat16)
    return np.stack([high, low])


def horner(coeffs, z):
    value = coeffs[-1] * z + coeffs[-2]
    for coeff in coeffs[-3::-1]:
        value = value * z + coeff
    return value


def split(value):
    high = value.astype(jnp.bfloat16)
    low = (value - high.astype(jnp.float32)).astype(jnp.bfloat16)
    return high, low


def dot_rows(left, right):
    return lax.dot_general(
        left, right, (((1,), (1,)), ((), ())), preferred_element_type=jnp.float32
    )


def fused_kernel(
    tm_size,
    pos_hbm,
    vel_hbm,
    species_hbm,
    wave_hbm,
    table_hbm,
    out_ref,
    pos_ref,
    vel_ref,
    species_ref,
    wave_ref,
    table,
    wave_cols,
    factor,
    weights,
    acc,
    modes,
    from_pair,
    summed,
    signals,
    result,
    result_in,
    load_sem,
    pair_send,
    pair_recv,
    peer_send,
    peer_recv,
    last_send,
    last_recv,
):
    me = lax.axis_index("tm")
    core = lax.axis_index("atom")
    other = 1 - core
    frames = pos_ref.shape[1]
    waves = wave_ref.shape[1]
    atoms = pos_ref.shape[2]
    groups = frames // GROUP
    frame_total = frames * tm_size
    early = GROUP // STEP // 2

    loads = [
        pltpu.make_async_copy(source, target, load_sem.at[n])
        for n, (source, target) in enumerate(
            (
                (wave_hbm, wave_ref),
                (species_hbm, species_ref),
                (vel_hbm, vel_ref),
                (pos_hbm, pos_ref),
                (table_hbm, table),
            )
        )
    ]
    for load in loads:
        load.start()
    barrier = pltpu.get_barrier_semaphore()
    for hop in range(1, tm_size):
        peer = lax.rem(me + hop, tm_size)
        pl.semaphore_signal(
            barrier, inc=1, device_id=(peer, core), device_id_type=pl.DeviceIdType.MESH
        )
    pl.semaphore_signal(
        barrier, inc=1, device_id=(me, other), device_id_type=pl.DeviceIdType.MESH
    )

    loads[0].wait()
    lane = lax.broadcasted_iota(jnp.int32, (waves, 128), 1)
    for d in range(3):
        row = wave_ref[d : d + 1, :].astype(jnp.float32)
        wave_cols[d] = jnp.broadcast_to(row, (128, waves)).T
    scaled = jnp.where(
        lane < 64, wave_cols[0], jnp.where(lane < 96, wave_cols[1], wave_cols[2])
    ) * (1.0 / WAVE_MAX)
    factor[...] = jnp.where(lane < 32, 1.0, scaled)
    for load in loads[1:4]:
        load.wait()
    species_b = species_ref[...].astype(jnp.float32)
    species_a = 1.0 - species_b

    def trig(t):
        turn = None
        for d in range(3):
            coord = pos_ref[d, pl.ds(t, 1), :].astype(jnp.float32) * (1.0 / 16384.0)
            wave = wave_cols[d]
            term = jnp.concatenate([wave] * (atoms // 128), 1) * coord
            turn = term if turn is None else turn + term
        magic = jnp.float32(12582912.0)
        rest = turn - ((turn + magic) - magic)
        z = rest * rest
        half_sin = rest * horner(SIN_COEFFS, z)
        return 1.0 - half_sin * half_sin, half_sin * horner(COS_COEFFS, z)

    def pair_copy(tg):
        return pltpu.make_async_remote_copy(
            src_ref=modes.at[tg, other],
            dst_ref=from_pair.at[tg],
            send_sem=pair_send.at[tg],
            recv_sem=pair_recv.at[tg],
            device_id=(me, other),
            device_id_type=pl.DeviceIdType.MESH,
        )

    def peer_copy(tg, hop):
        peer = lax.rem(me + hop, tm_size)
        return pltpu.make_async_remote_copy(
            src_ref=summed.at[tg, peer],
            dst_ref=signals.at[me, tg],
            send_sem=peer_send.at[tg, hop],
            recv_sem=peer_recv.at[tg, hop],
            device_id=(peer, core),
            device_id_type=pl.DeviceIdType.MESH,
        )

    def reduce_and_send(tg):
        pair_copy(tg).wait_recv()
        summed[tg] = modes[tg, core] + from_pair[tg]
        for hop in range(1, tm_size):
            peer_copy(tg, hop).start()
        signals[me, tg] = summed[tg, me]

    row_index = lax.broadcasted_iota(jnp.int32, (256, atoms), 0)
    for tg in range(groups):
        rows = []
        for q in range(4):
            for spec in (species_a, species_b):
                if q == 0:
                    rows.append(jnp.broadcast_to(spec, (GROUP, atoms)))
                else:
                    rows.append(vel_ref[q - 1, tg * GROUP : (tg + 1) * GROUP, :] * spec)
        kinds = jnp.concatenate(rows, 0)
        high, low = split(kinds)
        weights[0:128] = high.astype(jnp.float32)
        weights[128:256] = low.astype(jnp.float32)
        acc[...] = jnp.zeros_like(acc)

        def step(index, carry):
            left_cos, left_sin, right = [], [], []
            for k in range(STEP):
                local = index * STEP + k
                cosine, sine = trig(tg * GROUP + local)
                left_cos += list(split(cosine))
                left_sin += list(split(sine))
                frame_w = jnp.where(
                    (row_index & (GROUP - 1)) == local, weights[...], 0.0
                ).astype(jnp.bfloat16)
                right += [frame_w, frame_w]
            right = jnp.concatenate(right, 1)
            acc[0:waves] += dot_rows(jnp.concatenate(left_cos, 1), right)
            acc[waves : 2 * waves] += dot_rows(jnp.concatenate(left_sin, 1), right)
            return carry

        if tg > 0:
            lax.fori_loop(0, early, step, 0)
            reduce_and_send(tg - 1)
            lax.fori_loop(early, GROUP // STEP, step, 0)
        else:
            lax.fori_loop(0, GROUP // STEP, step, 0)
        halves = []
        for c in range(2):
            block = acc[c * waves : (c + 1) * waves]
            part = (block[:, :128] + block[:, 128:]) * factor[...]
            current = part + pltpu.roll(part, 96, 1) + pltpu.roll(part, 64, 1)
            halves.append(jnp.where(lane < 32, part, current))
        packed = jnp.where(lane < 64, halves[0], pltpu.roll(halves[1], 64, 1))
        packed = packed.reshape(tm_size, 2, 8, 128)
        modes[tg, 0] = packed[:, 0]
        modes[tg, 1] = packed[:, 1]
        if tg == 0:
            pl.semaphore_wait(barrier, tm_size)
        pair_copy(tg).start()
    reduce_and_send(groups - 1)
    loads[4].wait()
    for tg in range(groups):
        for hop in range(1, tm_size):
            peer_copy(tg, hop).wait_recv()

    tiles = signals[...].reshape(frame_total // 128, 8, 8, 128)
    wide = frame_total // 128 * 8
    group_lane = lax.broadcasted_iota(jnp.int32, (wide, 128), 1) // 16
    turned = [
        pltpu.roll(tiles[:, p].reshape(wide, 128), 16 * p, 1) if p else tiles[:, p].reshape(wide, 128)
        for p in range(8)
    ]
    rows = []
    for m in range(8):
        picked = turned[0]
        for p in range(1, 8):
            picked = jnp.where(group_lane == (m + p) % 8, turned[p], picked)
        if m:
            picked = pltpu.roll(picked, 128 - 16 * m, 1)
        rows.append(
            jnp.concatenate([picked[v * 8 : v * 8 + 8] for v in range(frame_total // 128)], 1)
        )
    high, low = split(jnp.concatenate(rows, 0))
    both = jnp.dot(
        jnp.concatenate([high, low], 0), table[0], preferred_element_type=jnp.float32
    )
    spectra = both[:64] + both[64:] + jnp.dot(high, table[1], preferred_element_type=jnp.float32)
    first = lax.broadcasted_iota(jnp.int32, (8, frame_total), 1) == 0
    out_rows = []
    for g in range(2):
        for a, b in ((0, 0), (0, 1), (1, 1)):
            even = jnp.zeros((8, frame_total), jnp.float32)
            odd = jnp.zeros((8, frame_total), jnp.float32)
            imag = jnp.zeros((8, frame_total), jnp.float32)
            for c in range(2):
                row_a = (c * 4 + g * 2 + a) * 8
                row_b = (c * 4 + g * 2 + b) * 8
                cos_a = spectra[row_a : row_a + 8, :frame_total]
                sin_a = spectra[row_a : row_a + 8, frame_total:]
                cos_b = spectra[row_b : row_b + 8, :frame_total]
                sin_b = spectra[row_b : row_b + 8, frame_total:]
                even += cos_a * cos_b
                odd += sin_a * sin_b
                imag += sin_a * cos_b - cos_a * sin_b
            real = jnp.where(first, even, 2.0 * (even + odd))
            imag = jnp.where(first, odd, 2.0 * imag)
            out_rows.append(jnp.concatenate([real, imag], 1))
    high, low = split(jnp.concatenate(out_rows, 0))
    lags = 2 * out_ref.shape[2]
    both = dot_rows(jnp.concatenate([high, low], 0), table[0, :lags])
    corr = both[:48] + both[48:] + dot_rows(high, table[1, :lags])
    lag = lax.broadcasted_iota(jnp.int32, (1, lags), 1)
    norm = 1.0 / (
        (frame_total - lag).astype(jnp.float32) * jnp.float32(2 * frame_total * 2 * atoms)
    )
    corr = (corr * norm).reshape(6, 8, lags)
    result[0] = corr[:, :, : lags // 2]
    result[1] = corr[:, :, lags // 2 :]
    swap = pltpu.make_async_remote_copy(
        src_ref=result.at[other],
        dst_ref=result_in,
        send_sem=last_send,
        recv_sem=last_recv,
        device_id=(me, other),
        device_id_type=pl.DeviceIdType.MESH,
    )
    swap.start()
    out_ref[:, pl.ds(pl.multiple_of(core * 8, 8), 8), :] = result[core]
    for tg in range(groups):
        pair_copy(tg).wait_send()
        for hop in range(1, tm_size):
            peer_copy(tg, hop).wait_send()
    swap.wait()
    out_ref[:, pl.ds(pl.multiple_of(other * 8, 8), 8), :] = result_in[...]


def per_device_fused(tm_size, positions, velocities, species, wave_vectors):
    frames, atoms = positions.shape[1:]
    waves = wave_vectors.shape[1]
    groups = frames // GROUP
    frame_total = frames * tm_size
    lag_here = frame_total // 4
    vmem = pl.BlockSpec(memory_space=pltpu.VMEM)
    dma = pltpu.SemaphoreType.DMA
    return pl.pallas_call(
        lambda *refs: fused_kernel(tm_size, *refs),
        name="scattering",
        out_shape=jax.ShapeDtypeStruct((6, 16, lag_here), jnp.float32),
        in_specs=[pl.BlockSpec(memory_space=pltpu.HBM)] * 5,
        out_specs=vmem,
        scratch_shapes=[
            pltpu.VMEM(positions.shape, jnp.int32),
            pltpu.VMEM(velocities.shape, jnp.float32),
            pltpu.VMEM((1, atoms), jnp.int32),
            pltpu.VMEM(wave_vectors.shape, jnp.int32),
            pltpu.VMEM((2, frame_total, 2 * frame_total), jnp.bfloat16),
            pltpu.VMEM((3, waves, 128), jnp.float32),
            pltpu.VMEM((waves, 128), jnp.float32),
            pltpu.VMEM((256, atoms), jnp.float32),
            pltpu.VMEM((2 * waves, 256), jnp.float32),
            pltpu.VMEM((groups, 2, tm_size, 8, 128), jnp.float32),
            pltpu.VMEM((groups, tm_size, 8, 128), jnp.float32),
            pltpu.VMEM((groups, tm_size, 8, 128), jnp.float32),
            pltpu.VMEM((tm_size, groups, 8, 128), jnp.float32),
            pltpu.VMEM((2, 6, 8, lag_here), jnp.float32),
            pltpu.VMEM((6, 8, lag_here), jnp.float32),
            dma((5,)),
            dma((groups,)),
            dma((groups,)),
            dma((groups, tm_size)),
            dma((groups, tm_size)),
            dma,
            dma,
        ],
        compiler_params=pltpu.CompilerParams(
            collective_id=0, has_side_effects=True, vmem_limit_bytes=48 << 20
        ),
    )(
        positions,
        velocities,
        species.reshape(1, atoms),
        wave_vectors,
        jnp.asarray(dft_tables(frame_total)),
    )


def solution(mesh):
    tm_size = mesh.shape["tm"]
    atom_size = mesh.shape["atom"]

    def per_device(positions, velocities, species, wave_vectors):
        frames, atoms = positions.shape[1:]
        waves = wave_vectors.shape[1]
        fits = (
            tm_size == 16
            and atom_size == 2
            and frames == 2 * GROUP
            and atoms == 256
            and waves == 256
        )
        if fits:
            return per_device_fused(tm_size, positions, velocities, species, wave_vectors)
        return per_device_general(positions, velocities, species, wave_vectors)

    return jax.shard_map(
        per_device,
        mesh=mesh,
        in_specs=(P(None, "tm", "atom"), P(None, "tm", "atom"), P("atom"), P()),
        out_specs=P(None, "tm", "atom"),
        check_vma=False,
    )
```

```python
import math

import jax
import jax.numpy as jnp
import ml_dtypes
import numpy as np
from jax import lax
from jax.experimental import pallas as pl
from jax.experimental.pallas import tpu as pltpu
from jax.sharding import PartitionSpec as P

WAVE_MAX = 64


highest = lax.Precision.HIGHEST


def frame_block(pos_block, vel_block, species_onehot, wave_vectors):
    summed = (
        pos_block[0][:, :, None] * wave_vectors[0]
        + pos_block[1][:, :, None] * wave_vectors[1]
        + pos_block[2][:, :, None] * wave_vectors[2]
    )
    angle_unit = jnp.float32(2.0 * math.pi / 16384.0)
    phase = jnp.remainder(summed, 16384).astype(jnp.float32) * angle_unit
    kinds = jnp.concatenate([jnp.ones_like(vel_block[:1]), vel_block], 0)
    weights = kinds[:, None] * species_onehot[None, :, None, :]
    cos_part = jnp.einsum("qsba,bak->qsbk", weights, jnp.cos(phase), precision=highest)
    sin_part = jnp.einsum("qsba,bak->qsbk", weights, jnp.sin(phase), precision=highest)
    return jnp.stack([cos_part, sin_part])


def pair_terms(cos_rows, sin_rows):
    cos_a = cos_rows[:, :, 0]
    cos_b = cos_rows[:, :, 1]
    sin_a = sin_rows[:, :, 0]
    sin_b = sin_rows[:, :, 1]
    real_part = jnp.stack(
        [
            cos_a * cos_a + sin_a * sin_a,
            cos_a * cos_b + sin_a * sin_b,
            cos_b * cos_b + sin_b * sin_b,
        ],
        2,
    ).sum(0)
    imag_part = jnp.stack(
        [
            cos_a * sin_a - sin_a * cos_a,
            cos_a * sin_b - sin_a * cos_b,
            cos_b * sin_b - sin_b * cos_b,
        ],
        2,
    ).sum(0)
    return (real_part, imag_part)


def correlate(signals, atom_total):
    frame_total = signals.shape[-1]
    waves_here = signals.shape[3]
    signal_rows = signals.reshape(-1, frame_total)
    groups = lax.axis_size("atom")
    freq_count = frame_total // groups
    lag_count = frame_total // 2 // groups
    my_index = lax.axis_index("atom")
    freq_index = my_index * freq_count + jnp.arange(freq_count, dtype=jnp.int32)
    time_index = jnp.arange(frame_total, dtype=jnp.int32)
    angle_step = jnp.float32(math.pi / frame_total)
    turns = jnp.remainder(time_index[:, None] * freq_index[None, :], 2 * frame_total)
    angles = turns.astype(jnp.float32) * angle_step
    spec_cos = jnp.dot(signal_rows, jnp.cos(angles), precision=highest).reshape(
        2, 2, 2, waves_here, freq_count
    )
    spec_sin = jnp.dot(signal_rows, jnp.sin(angles), precision=highest).reshape(
        2, 2, 2, waves_here, freq_count
    )
    real_part, imag_part = pair_terms(spec_cos, spec_sin)
    spectral_weight = jnp.where(freq_index == 0, 1.0, 2.0).astype(jnp.float32)
    real_rows = (real_part * spectral_weight).reshape(6 * waves_here, freq_count)
    imag_rows = (imag_part * spectral_weight).reshape(6 * waves_here, freq_count)
    alternating = jnp.where(time_index % 2 == 0, 1.0, -1.0).astype(jnp.float32)
    nyquist = jnp.dot(signal_rows, alternating, precision=highest).reshape(2, 2, 2, waves_here)
    nyq_a = nyquist[:, :, 0]
    nyq_b = nyquist[:, :, 1]
    nyq_real = (
        jnp.stack([nyq_a * nyq_a, nyq_a * nyq_b, nyq_b * nyq_b], 2).sum(0).reshape(6 * waves_here)
    )
    nyq_here = nyq_real * jnp.where(my_index == 0, 1.0, 0.0).astype(jnp.float32)
    lag_index = jnp.arange(lag_count * lax.axis_size("atom"), dtype=jnp.int32)
    lag_turns = jnp.remainder(lag_index[:, None] * freq_index[None, :], 2 * frame_total)
    lag_angles = lag_turns.astype(jnp.float32) * angle_step
    term = jnp.dot(jnp.cos(lag_angles), real_rows.T, precision=highest) - jnp.dot(
        jnp.sin(lag_angles), imag_rows.T, precision=highest
    )
    lag_sign = jnp.where(lag_index % 2 == 0, 1.0, -1.0).astype(jnp.float32)
    shared = lax.psum_scatter(
        term + lag_sign[:, None] * nyq_here[None, :], "atom", scatter_dimension=0, tiled=True
    )
    lag_index = my_index * lag_count + jnp.arange(lag_count, dtype=jnp.int32)
    scaled = shared / jnp.float32(2 * frame_total)
    isf = (
        scaled / (jnp.float32(atom_total) * (frame_total - lag_index).astype(jnp.float32))[:, None]
    )
    return isf.T.reshape(6, waves_here, lag_count)


def per_device_general(positions, velocities, species, wave_vectors):
    atom_count = positions.shape[2]
    frame_count = positions.shape[1]
    wave_count = wave_vectors.shape[1]
    block_size = math.gcd(frame_count, 2)
    block_count = frame_count // block_size
    species_onehot = jnp.stack([1 - species, species]).astype(jnp.float32)
    pos_blocks = positions.reshape(3, block_count, block_size, atom_count).transpose(1, 0, 2, 3)
    vel_blocks = velocities.reshape(3, block_count, block_size, atom_count).transpose(1, 0, 2, 3)
    raw_modes = lax.map(
        lambda operands: frame_block(operands[0], operands[1], species_onehot, wave_vectors),
        (pos_blocks, vel_blocks),
    )
    raw_modes = raw_modes.transpose(1, 2, 3, 0, 4, 5).reshape(2, 4, 2, frame_count, wave_count)
    wave_scaled = wave_vectors.astype(jnp.float32) / WAVE_MAX
    current = (
        wave_scaled[0] * raw_modes[:, 1]
        + wave_scaled[1] * raw_modes[:, 2]
        + wave_scaled[2] * raw_modes[:, 3]
    )
    modes = jnp.stack([raw_modes[:, 0], current], 1)
    atom_groups = lax.axis_size("atom")
    summed = lax.psum(modes, "atom")
    owned = lax.all_to_all(summed, "tm", split_axis=4, concat_axis=3, tiled=True)
    signals = jnp.moveaxis(owned, 3, 4)
    return correlate(signals, atom_count * atom_groups)


GROUP = 16
STEP = 8


def even_coeffs(func, degree):
    fit = np.polynomial.chebyshev.Chebyshev.interpolate(
        lambda z: func(np.sqrt(np.maximum(z, 1e-12))), degree, domain=[0.0, 0.25]
    )
    return [float(v) for v in fit.convert(kind=np.polynomial.Polynomial).coef]


COS_COEFFS = even_coeffs(lambda r: np.sqrt(2.0) * np.cos(np.pi * r), 3)
SIN_COEFFS = even_coeffs(lambda r: np.sqrt(2.0) * np.sin(np.pi * r) / r, 3)


def dft_tables(frames):
    turns = np.outer(np.arange(frames), np.arange(frames)) % (2 * frames)
    angle = turns * (np.pi / frames)
    sine = np.sin(angle)
    sine[:, 0] = 1.0 - 2.0 * (np.arange(frames) % 2)
    table = np.concatenate([np.cos(angle), sine], 1).astype(np.float32)
    high = table.astype(ml_dtypes.bfloat16)
    low = (table - high.astype(np.float32)).astype(ml_dtypes.bfloat16)
    return np.stack([high, low])


def horner(coeffs, z):
    value = coeffs[-1] * z + coeffs[-2]
    for coeff in coeffs[-3::-1]:
        value = value * z + coeff
    return value


def split(value):
    high = value.astype(jnp.bfloat16)
    low = (value - high.astype(jnp.float32)).astype(jnp.bfloat16)
    return high, low


def dot_rows(left, right):
    return lax.dot_general(
        left, right, (((1,), (1,)), ((), ())), preferred_element_type=jnp.float32
    )


def fused_kernel(
    tm_size,
    pos_hbm,
    vel_hbm,
    species_hbm,
    wave_hbm,
    table_hbm,
    out_ref,
    pos_ref,
    vel_ref,
    species_ref,
    wave_ref,
    table,
    wave_cols,
    factor,
    weights,
    acc,
    modes,
    from_pair,
    summed,
    signals,
    result,
    result_in,
    load_sem,
    pair_send,
    pair_recv,
    peer_send,
    peer_recv,
    last_send,
    last_recv,
):
    me = lax.axis_index("tm")
    core = lax.axis_index("atom")
    other = 1 - core
    frames = pos_ref.shape[1]
    waves = wave_ref.shape[1]
    atoms = pos_ref.shape[2]
    groups = frames // GROUP
    frame_total = frames * tm_size
    early = GROUP // STEP // 2

    loads = [
        pltpu.make_async_copy(source, target, load_sem.at[n])
        for n, (source, target) in enumerate(
            (
                (wave_hbm, wave_ref),
                (species_hbm, species_ref),
                (vel_hbm, vel_ref),
                (pos_hbm, pos_ref),
                (table_hbm, table),
            )
        )
    ]
    for load in loads:
        load.start()
    barrier = pltpu.get_barrier_semaphore()
    for hop in range(1, tm_size):
        peer = lax.rem(me + hop, tm_size)
        pl.semaphore_signal(
            barrier, inc=1, device_id=(peer, core), device_id_type=pl.DeviceIdType.MESH
        )
    pl.semaphore_signal(
        barrier, inc=1, device_id=(me, other), device_id_type=pl.DeviceIdType.MESH
    )

    loads[0].wait()
    lane = lax.broadcasted_iota(jnp.int32, (waves, 128), 1)
    for d in range(3):
        row = wave_ref[d : d + 1, :].astype(jnp.float32)
        wave_cols[d] = jnp.broadcast_to(row, (128, waves)).T
    scaled = jnp.where(
        lane < 64, wave_cols[0], jnp.where(lane < 96, wave_cols[1], wave_cols[2])
    ) * (1.0 / WAVE_MAX)
    factor[...] = jnp.where(lane < 32, 1.0, scaled)
    for load in loads[1:4]:
        load.wait()
    species_b = species_ref[...].astype(jnp.float32)
    species_a = 1.0 - species_b

    def trig(t):
        turn = None
        for d in range(3):
            coord = pos_ref[d, pl.ds(t, 1), :].astype(jnp.float32) * (1.0 / 16384.0)
            wave = wave_cols[d]
            term = jnp.concatenate([wave] * (atoms // 128), 1) * coord
            turn = term if turn is None else turn + term
        magic = jnp.float32(12582912.0)
        rest = turn - ((turn + magic) - magic)
        z = rest * rest
        half_sin = rest * horner(SIN_COEFFS, z)
        return 1.0 - half_sin * half_sin, half_sin * horner(COS_COEFFS, z)

    def pair_copy(tg):
        return pltpu.make_async_remote_copy(
            src_ref=modes.at[tg, other],
            dst_ref=from_pair.at[tg],
            send_sem=pair_send.at[tg],
            recv_sem=pair_recv.at[tg],
            device_id=(me, other),
            device_id_type=pl.DeviceIdType.MESH,
        )

    def peer_copy(tg, hop):
        peer = lax.rem(me + hop, tm_size)
        return pltpu.make_async_remote_copy(
            src_ref=summed.at[tg, peer],
            dst_ref=signals.at[me, tg],
            send_sem=peer_send.at[tg, hop],
            recv_sem=peer_recv.at[tg, hop],
            device_id=(peer, core),
            device_id_type=pl.DeviceIdType.MESH,
        )

    def reduce_and_send(tg):
        pair_copy(tg).wait_recv()
        summed[tg] = modes[tg, core] + from_pair[tg]
        for hop in range(1, tm_size):
            peer_copy(tg, hop).start()
        signals[me, tg] = summed[tg, me]

    row_index = lax.broadcasted_iota(jnp.int32, (256, atoms), 0)
    def group(tg, carry):
        rows = []
        for q in range(4):
            for spec in (species_a, species_b):
                if q == 0:
                    rows.append(jnp.broadcast_to(spec, (GROUP, atoms)))
                else:
                    rows.append(vel_ref[q - 1, pl.ds(pl.multiple_of(tg * GROUP, GROUP), GROUP), :] * spec)
        kinds = jnp.concatenate(rows, 0)
        high, low = split(kinds)
        weights[0:128] = high.astype(jnp.float32)
        weights[128:256] = low.astype(jnp.float32)
        acc[...] = jnp.zeros_like(acc)

        def step(index, carry):
            @pl.when(jnp.logical_and(tg == 0, index == GROUP // STEP - 1))
            def _():
                pl.semaphore_wait(barrier, tm_size)

            @pl.when(jnp.logical_and(tg > 0, index == early))
            def _():
                reduce_and_send(tg - 1)

            left_cos, left_sin, right = [], [], []
            for k in range(STEP):
                local = index * STEP + k
                cosine, sine = trig(tg * GROUP + local)
                left_cos += list(split(cosine))
                left_sin += list(split(sine))
                frame_w = jnp.where(
                    (row_index & (GROUP - 1)) == local, weights[...], 0.0
                ).astype(jnp.bfloat16)
                right += [frame_w, frame_w]
            right = jnp.concatenate(right, 1)
            acc[0:waves] += dot_rows(jnp.concatenate(left_cos, 1), right)
            acc[waves : 2 * waves] += dot_rows(jnp.concatenate(left_sin, 1), right)
            return carry

        lax.fori_loop(0, GROUP // STEP, step, 0)
        halves = []
        for c in range(2):
            block = acc[c * waves : (c + 1) * waves]
            part = (block[:, :128] + block[:, 128:]) * factor[...]
            current = part + pltpu.roll(part, 96, 1) + pltpu.roll(part, 64, 1)
            halves.append(jnp.where(lane < 32, part, current))
        packed = jnp.where(lane < 64, halves[0], pltpu.roll(halves[1], 64, 1))
        packed = packed.reshape(tm_size, 2, 8, 128)
        modes[tg, 0] = packed[:, 0]
        modes[tg, 1] = packed[:, 1]
        pair_copy(tg).start()
        return carry

    lax.fori_loop(0, groups, group, 0)
    reduce_and_send(groups - 1)
    loads[4].wait()
    for tg in range(groups):
        for hop in range(1, tm_size):
            peer_copy(tg, hop).wait_recv()

    tiles = signals[...].reshape(frame_total // 128, 8, 8, 128)
    wide = frame_total // 128 * 8
    group_lane = lax.broadcasted_iota(jnp.int32, (wide, 128), 1) // 16
    turned = [
        pltpu.roll(tiles[:, p].reshape(wide, 128), 16 * p, 1) if p else tiles[:, p].reshape(wide, 128)
        for p in range(8)
    ]
    rows = []
    for m in range(8):
        picked = turned[0]
        for p in range(1, 8):
            picked = jnp.where(group_lane == (m + p) % 8, turned[p], picked)
        if m:
            picked = pltpu.roll(picked, 128 - 16 * m, 1)
        rows.append(
            jnp.concatenate([picked[v * 8 : v * 8 + 8] for v in range(frame_total // 128)], 1)
        )
    high, low = split(jnp.concatenate(rows, 0))
    both = jnp.dot(
        jnp.concatenate([high, low], 0), table[0], preferred_element_type=jnp.float32
    )
    spectra = both[:64] + both[64:] + jnp.dot(high, table[1], preferred_element_type=jnp.float32)
    first = lax.broadcasted_iota(jnp.int32, (8, frame_total), 1) == 0
    out_rows = []
    for g in range(2):
        for a, b in ((0, 0), (0, 1), (1, 1)):
            even = jnp.zeros((8, frame_total), jnp.float32)
            odd = jnp.zeros((8, frame_total), jnp.float32)
            imag = jnp.zeros((8, frame_total), jnp.float32)
            for c in range(2):
                row_a = (c * 4 + g * 2 + a) * 8
                row_b = (c * 4 + g * 2 + b) * 8
                cos_a = spectra[row_a : row_a + 8, :frame_total]
                sin_a = spectra[row_a : row_a + 8, frame_total:]
                cos_b = spectra[row_b : row_b + 8, :frame_total]
                sin_b = spectra[row_b : row_b + 8, frame_total:]
                even += cos_a * cos_b
                odd += sin_a * sin_b
                imag += sin_a * cos_b - cos_a * sin_b
            real = jnp.where(first, even, 2.0 * (even + odd))
            imag = jnp.where(first, odd, 2.0 * imag)
            out_rows.append(jnp.concatenate([real, imag], 1))
    high, low = split(jnp.concatenate(out_rows, 0))
    lags = 2 * out_ref.shape[2]
    both = dot_rows(jnp.concatenate([high, low], 0), table[0, :lags])
    corr = both[:48] + both[48:] + dot_rows(high, table[1, :lags])
    lag = lax.broadcasted_iota(jnp.int32, (1, lags), 1)
    norm = 1.0 / (
        (frame_total - lag).astype(jnp.float32) * jnp.float32(2 * frame_total * 2 * atoms)
    )
    corr = (corr * norm).reshape(6, 8, lags)
    result[0] = corr[:, :, : lags // 2]
    result[1] = corr[:, :, lags // 2 :]
    swap = pltpu.make_async_remote_copy(
        src_ref=result.at[other],
        dst_ref=result_in,
        send_sem=last_send,
        recv_sem=last_recv,
        device_id=(me, other),
        device_id_type=pl.DeviceIdType.MESH,
    )
    swap.start()
    out_ref[:, pl.ds(pl.multiple_of(core * 8, 8), 8), :] = result[core]
    for tg in range(groups):
        pair_copy(tg).wait_send()
        for hop in range(1, tm_size):
            peer_copy(tg, hop).wait_send()
    swap.wait()
    out_ref[:, pl.ds(pl.multiple_of(other * 8, 8), 8), :] = result_in[...]


def per_device_fused(tm_size, positions, velocities, species, wave_vectors):
    frames, atoms = positions.shape[1:]
    waves = wave_vectors.shape[1]
    groups = frames // GROUP
    frame_total = frames * tm_size
    lag_here = frame_total // 4
    vmem = pl.BlockSpec(memory_space=pltpu.VMEM)
    dma = pltpu.SemaphoreType.DMA
    return pl.pallas_call(
        lambda *refs: fused_kernel(tm_size, *refs),
        name="scattering",
        out_shape=jax.ShapeDtypeStruct((6, 16, lag_here), jnp.float32),
        in_specs=[pl.BlockSpec(memory_space=pltpu.HBM)] * 5,
        out_specs=vmem,
        scratch_shapes=[
            pltpu.VMEM(positions.shape, jnp.int32),
            pltpu.VMEM(velocities.shape, jnp.float32),
            pltpu.VMEM((1, atoms), jnp.int32),
            pltpu.VMEM(wave_vectors.shape, jnp.int32),
            pltpu.VMEM((2, frame_total, 2 * frame_total), jnp.bfloat16),
            pltpu.VMEM((3, waves, 128), jnp.float32),
            pltpu.VMEM((waves, 128), jnp.float32),
            pltpu.VMEM((256, atoms), jnp.float32),
            pltpu.VMEM((2 * waves, 256), jnp.float32),
            pltpu.VMEM((groups, 2, tm_size, 8, 128), jnp.float32),
            pltpu.VMEM((groups, tm_size, 8, 128), jnp.float32),
            pltpu.VMEM((groups, tm_size, 8, 128), jnp.float32),
            pltpu.VMEM((tm_size, groups, 8, 128), jnp.float32),
            pltpu.VMEM((2, 6, 8, lag_here), jnp.float32),
            pltpu.VMEM((6, 8, lag_here), jnp.float32),
            dma((5,)),
            dma((groups,)),
            dma((groups,)),
            dma((groups, tm_size)),
            dma((groups, tm_size)),
            dma,
            dma,
        ],
        compiler_params=pltpu.CompilerParams(
            collective_id=0, has_side_effects=True, vmem_limit_bytes=48 << 20
        ),
    )(
        positions,
        velocities,
        species.reshape(1, atoms),
        wave_vectors,
        jnp.asarray(dft_tables(frame_total)),
    )


def solution(mesh):
    tm_size = mesh.shape["tm"]
    atom_size = mesh.shape["atom"]

    def per_device(positions, velocities, species, wave_vectors):
        frames, atoms = positions.shape[1:]
        waves = wave_vectors.shape[1]
        fits = (
            tm_size == 16
            and atom_size == 2
            and frames == 2 * GROUP
            and atoms == 256
            and waves == 256
        )
        if fits:
            return per_device_fused(tm_size, positions, velocities, species, wave_vectors)
        return per_device_general(positions, velocities, species, wave_vectors)

    return jax.shard_map(
        per_device,
        mesh=mesh,
        in_specs=(P(None, "tm", "atom"), P(None, "tm", "atom"), P("atom"), P()),
        out_specs=P(None, "tm", "atom"),
        check_vma=False,
    )
```

```python
import math

import jax
import jax.numpy as jnp
import ml_dtypes
import numpy as np
from jax import lax
from jax.experimental import pallas as pl
from jax.experimental.pallas import tpu as pltpu
from jax.sharding import PartitionSpec as P

WAVE_MAX = 64


highest = lax.Precision.HIGHEST


def frame_block(pos_block, vel_block, species_onehot, wave_vectors):
    summed = (
        pos_block[0][:, :, None] * wave_vectors[0]
        + pos_block[1][:, :, None] * wave_vectors[1]
        + pos_block[2][:, :, None] * wave_vectors[2]
    )
    angle_unit = jnp.float32(2.0 * math.pi / 16384.0)
    phase = jnp.remainder(summed, 16384).astype(jnp.float32) * angle_unit
    kinds = jnp.concatenate([jnp.ones_like(vel_block[:1]), vel_block], 0)
    weights = kinds[:, None] * species_onehot[None, :, None, :]
    cos_part = jnp.einsum("qsba,bak->qsbk", weights, jnp.cos(phase), precision=highest)
    sin_part = jnp.einsum("qsba,bak->qsbk", weights, jnp.sin(phase), precision=highest)
    return jnp.stack([cos_part, sin_part])


def pair_terms(cos_rows, sin_rows):
    cos_a = cos_rows[:, :, 0]
    cos_b = cos_rows[:, :, 1]
    sin_a = sin_rows[:, :, 0]
    sin_b = sin_rows[:, :, 1]
    real_part = jnp.stack(
        [
            cos_a * cos_a + sin_a * sin_a,
            cos_a * cos_b + sin_a * sin_b,
            cos_b * cos_b + sin_b * sin_b,
        ],
        2,
    ).sum(0)
    imag_part = jnp.stack(
        [
            cos_a * sin_a - sin_a * cos_a,
            cos_a * sin_b - sin_a * cos_b,
            cos_b * sin_b - sin_b * cos_b,
        ],
        2,
    ).sum(0)
    return (real_part, imag_part)


def correlate(signals, atom_total):
    frame_total = signals.shape[-1]
    waves_here = signals.shape[3]
    signal_rows = signals.reshape(-1, frame_total)
    groups = lax.axis_size("atom")
    freq_count = frame_total // groups
    lag_count = frame_total // 2 // groups
    my_index = lax.axis_index("atom")
    freq_index = my_index * freq_count + jnp.arange(freq_count, dtype=jnp.int32)
    time_index = jnp.arange(frame_total, dtype=jnp.int32)
    angle_step = jnp.float32(math.pi / frame_total)
    turns = jnp.remainder(time_index[:, None] * freq_index[None, :], 2 * frame_total)
    angles = turns.astype(jnp.float32) * angle_step
    spec_cos = jnp.dot(signal_rows, jnp.cos(angles), precision=highest).reshape(
        2, 2, 2, waves_here, freq_count
    )
    spec_sin = jnp.dot(signal_rows, jnp.sin(angles), precision=highest).reshape(
        2, 2, 2, waves_here, freq_count
    )
    real_part, imag_part = pair_terms(spec_cos, spec_sin)
    spectral_weight = jnp.where(freq_index == 0, 1.0, 2.0).astype(jnp.float32)
    real_rows = (real_part * spectral_weight).reshape(6 * waves_here, freq_count)
    imag_rows = (imag_part * spectral_weight).reshape(6 * waves_here, freq_count)
    alternating = jnp.where(time_index % 2 == 0, 1.0, -1.0).astype(jnp.float32)
    nyquist = jnp.dot(signal_rows, alternating, precision=highest).reshape(2, 2, 2, waves_here)
    nyq_a = nyquist[:, :, 0]
    nyq_b = nyquist[:, :, 1]
    nyq_real = (
        jnp.stack([nyq_a * nyq_a, nyq_a * nyq_b, nyq_b * nyq_b], 2).sum(0).reshape(6 * waves_here)
    )
    nyq_here = nyq_real * jnp.where(my_index == 0, 1.0, 0.0).astype(jnp.float32)
    lag_index = jnp.arange(lag_count * lax.axis_size("atom"), dtype=jnp.int32)
    lag_turns = jnp.remainder(lag_index[:, None] * freq_index[None, :], 2 * frame_total)
    lag_angles = lag_turns.astype(jnp.float32) * angle_step
    term = jnp.dot(jnp.cos(lag_angles), real_rows.T, precision=highest) - jnp.dot(
        jnp.sin(lag_angles), imag_rows.T, precision=highest
    )
    lag_sign = jnp.where(lag_index % 2 == 0, 1.0, -1.0).astype(jnp.float32)
    shared = lax.psum_scatter(
        term + lag_sign[:, None] * nyq_here[None, :], "atom", scatter_dimension=0, tiled=True
    )
    lag_index = my_index * lag_count + jnp.arange(lag_count, dtype=jnp.int32)
    scaled = shared / jnp.float32(2 * frame_total)
    isf = (
        scaled / (jnp.float32(atom_total) * (frame_total - lag_index).astype(jnp.float32))[:, None]
    )
    return isf.T.reshape(6, waves_here, lag_count)


def per_device_general(positions, velocities, species, wave_vectors):
    atom_count = positions.shape[2]
    frame_count = positions.shape[1]
    wave_count = wave_vectors.shape[1]
    block_size = math.gcd(frame_count, 2)
    block_count = frame_count // block_size
    species_onehot = jnp.stack([1 - species, species]).astype(jnp.float32)
    pos_blocks = positions.reshape(3, block_count, block_size, atom_count).transpose(1, 0, 2, 3)
    vel_blocks = velocities.reshape(3, block_count, block_size, atom_count).transpose(1, 0, 2, 3)
    raw_modes = lax.map(
        lambda operands: frame_block(operands[0], operands[1], species_onehot, wave_vectors),
        (pos_blocks, vel_blocks),
    )
    raw_modes = raw_modes.transpose(1, 2, 3, 0, 4, 5).reshape(2, 4, 2, frame_count, wave_count)
    wave_scaled = wave_vectors.astype(jnp.float32) / WAVE_MAX
    current = (
        wave_scaled[0] * raw_modes[:, 1]
        + wave_scaled[1] * raw_modes[:, 2]
        + wave_scaled[2] * raw_modes[:, 3]
    )
    modes = jnp.stack([raw_modes[:, 0], current], 1)
    atom_groups = lax.axis_size("atom")
    summed = lax.psum(modes, "atom")
    owned = lax.all_to_all(summed, "tm", split_axis=4, concat_axis=3, tiled=True)
    signals = jnp.moveaxis(owned, 3, 4)
    return correlate(signals, atom_count * atom_groups)


GROUP = 16
STEP = 8


def even_coeffs(func, degree):
    fit = np.polynomial.chebyshev.Chebyshev.interpolate(
        lambda z: func(np.sqrt(np.maximum(z, 1e-12))), degree, domain=[0.0, 0.25]
    )
    return [float(v) for v in fit.convert(kind=np.polynomial.Polynomial).coef]


COS_COEFFS = even_coeffs(lambda r: np.sqrt(2.0) * np.cos(np.pi * r), 3)
SIN_COEFFS = even_coeffs(lambda r: np.sqrt(2.0) * np.sin(np.pi * r) / r, 3)


def dft_tables(frames):
    turns = np.outer(np.arange(frames), np.arange(frames)) % (2 * frames)
    angle = turns * (np.pi / frames)
    sine = np.sin(angle)
    sine[:, 0] = 1.0 - 2.0 * (np.arange(frames) % 2)
    table = np.concatenate([np.cos(angle), sine], 1).astype(np.float32)
    high = table.astype(ml_dtypes.bfloat16)
    low = (table - high.astype(np.float32)).astype(ml_dtypes.bfloat16)
    return np.stack([high, low])


def horner(coeffs, z):
    value = coeffs[-1] * z + coeffs[-2]
    for coeff in coeffs[-3::-1]:
        value = value * z + coeff
    return value


def split(value):
    high = value.astype(jnp.bfloat16)
    low = (value - high.astype(jnp.float32)).astype(jnp.bfloat16)
    return high, low


def dot_rows(left, right):
    return lax.dot_general(
        left, right, (((1,), (1,)), ((), ())), preferred_element_type=jnp.float32
    )


def fused_kernel(
    tm_size,
    pos_hbm,
    vel_hbm,
    species_hbm,
    wave_hbm,
    table_hbm,
    out_ref,
    pos_ref,
    vel_ref,
    species_ref,
    wave_ref,
    table,
    wave_cols,
    factor,
    weights,
    acc,
    modes,
    from_pair,
    summed,
    signals,
    result,
    result_in,
    load_sem,
    pair_send,
    pair_recv,
    peer_send,
    peer_recv,
    last_send,
    last_recv,
):
    me = lax.axis_index("tm")
    core = lax.axis_index("atom")
    other = 1 - core
    frames = pos_ref.shape[1]
    waves = wave_ref.shape[1]
    atoms = pos_ref.shape[2]
    groups = frames // GROUP
    frame_total = frames * tm_size
    early = GROUP // STEP // 2

    loads = [
        pltpu.make_async_copy(source, target, load_sem.at[n])
        for n, (source, target) in enumerate(
            (
                (wave_hbm, wave_ref),
                (species_hbm, species_ref),
                (vel_hbm, vel_ref),
                (pos_hbm, pos_ref),
                (table_hbm, table),
            )
        )
    ]
    for load in loads:
        load.start()
    barrier = pltpu.get_barrier_semaphore()
    for hop in range(1, tm_size):
        peer = lax.rem(me + hop, tm_size)
        pl.semaphore_signal(
            barrier, inc=1, device_id=(peer, core), device_id_type=pl.DeviceIdType.MESH
        )
    pl.semaphore_signal(
        barrier, inc=1, device_id=(me, other), device_id_type=pl.DeviceIdType.MESH
    )

    loads[0].wait()
    lane = lax.broadcasted_iota(jnp.int32, (waves, 128), 1)
    for d in range(3):
        row = wave_ref[d : d + 1, :].astype(jnp.float32)
        wave_cols[d] = jnp.broadcast_to(row, (128, waves)).T
    scaled = jnp.where(
        lane < 64, wave_cols[0], jnp.where(lane < 96, wave_cols[1], wave_cols[2])
    ) * (1.0 / WAVE_MAX)
    factor[...] = jnp.where(lane < 32, 1.0, scaled)
    for load in loads[1:4]:
        load.wait()
    species_b = species_ref[...].astype(jnp.float32)
    species_a = 1.0 - species_b

    def trig(t):
        turn = None
        for d in range(3):
            coord = pos_ref[d, pl.ds(t, 1), :].astype(jnp.float32) * (1.0 / 16384.0)
            wave = wave_cols[d]
            term = jnp.concatenate([wave] * (atoms // 128), 1) * coord
            turn = term if turn is None else turn + term
        rest = turn - jnp.round(turn)
        z = rest * rest
        half_sin = rest * horner(SIN_COEFFS, z)
        return 1.0 - half_sin * half_sin, half_sin * horner(COS_COEFFS, z)

    def pair_copy(tg):
        return pltpu.make_async_remote_copy(
            src_ref=modes.at[tg, other],
            dst_ref=from_pair.at[tg],
            send_sem=pair_send.at[tg],
            recv_sem=pair_recv.at[tg],
            device_id=(me, other),
            device_id_type=pl.DeviceIdType.MESH,
        )

    def peer_copy(tg, hop):
        peer = lax.rem(me + hop, tm_size)
        return pltpu.make_async_remote_copy(
            src_ref=summed.at[tg, peer],
            dst_ref=signals.at[me, tg],
            send_sem=peer_send.at[tg, hop],
            recv_sem=peer_recv.at[tg, hop],
            device_id=(peer, core),
            device_id_type=pl.DeviceIdType.MESH,
        )

    def reduce_and_send(tg):
        pair_copy(tg).wait_recv()
        summed[tg] = modes[tg, core] + from_pair[tg]
        for hop in range(1, tm_size):
            peer_copy(tg, hop).start()
        signals[me, tg] = summed[tg, me]

    row_index = lax.broadcasted_iota(jnp.int32, (256, atoms), 0)
    def group(tg, carry):
        rows = []
        for q in range(4):
            for spec in (species_a, species_b):
                if q == 0:
                    rows.append(jnp.broadcast_to(spec, (GROUP, atoms)))
                else:
                    rows.append(vel_ref[q - 1, pl.ds(pl.multiple_of(tg * GROUP, GROUP), GROUP), :] * spec)
        kinds = jnp.concatenate(rows, 0)
        high, low = split(kinds)
        weights[0:128] = high.astype(jnp.float32)
        weights[128:256] = low.astype(jnp.float32)
        acc[...] = jnp.zeros_like(acc)

        def step(index, carry):
            @pl.when(jnp.logical_and(tg == 0, index == GROUP // STEP - 1))
            def _():
                pl.semaphore_wait(barrier, tm_size)

            @pl.when(jnp.logical_and(tg > 0, index == early))
            def _():
                reduce_and_send(tg - 1)

            left_cos, left_sin, right = [], [], []
            for k in range(STEP):
                local = index * STEP + k
                cosine, sine = trig(tg * GROUP + local)
                left_cos += list(split(cosine))
                left_sin += list(split(sine))
                frame_w = jnp.where(
                    (row_index & (GROUP - 1)) == local, weights[...], 0.0
                ).astype(jnp.bfloat16)
                right += [frame_w, frame_w]
            right = jnp.concatenate(right, 1)
            acc[0:waves] += dot_rows(jnp.concatenate(left_cos, 1), right)
            acc[waves : 2 * waves] += dot_rows(jnp.concatenate(left_sin, 1), right)
            return carry

        lax.fori_loop(0, GROUP // STEP, step, 0)
        halves = []
        for c in range(2):
            block = acc[c * waves : (c + 1) * waves]
            part = (block[:, :128] + block[:, 128:]) * factor[...]
            current = part + pltpu.roll(part, 96, 1) + pltpu.roll(part, 64, 1)
            halves.append(jnp.where(lane < 32, part, current))
        packed = jnp.where(lane < 64, halves[0], pltpu.roll(halves[1], 64, 1))
        packed = packed.reshape(tm_size, 2, 8, 128)
        modes[tg, 0] = packed[:, 0]
        modes[tg, 1] = packed[:, 1]
        pair_copy(tg).start()
        return carry

    lax.fori_loop(0, groups, group, 0)
    reduce_and_send(groups - 1)
    loads[4].wait()
    for tg in range(groups):
        for hop in range(1, tm_size):
            peer_copy(tg, hop).wait_recv()

    tiles = signals[...].reshape(frame_total // 128, 8, 8, 128)
    wide = frame_total // 128 * 8
    group_lane = lax.broadcasted_iota(jnp.int32, (wide, 128), 1) // 16
    turned = [
        pltpu.roll(tiles[:, p].reshape(wide, 128), 16 * p, 1) if p else tiles[:, p].reshape(wide, 128)
        for p in range(8)
    ]
    rows = []
    for m in range(8):
        picked = turned[0]
        for p in range(1, 8):
            picked = jnp.where(group_lane == (m + p) % 8, turned[p], picked)
        if m:
            picked = pltpu.roll(picked, 128 - 16 * m, 1)
        rows.append(
            jnp.concatenate([picked[v * 8 : v * 8 + 8] for v in range(frame_total // 128)], 1)
        )
    high, low = split(jnp.concatenate(rows, 0))
    both = jnp.dot(
        jnp.concatenate([high, low], 0), table[0], preferred_element_type=jnp.float32
    )
    spectra = both[:64] + both[64:] + jnp.dot(high, table[1], preferred_element_type=jnp.float32)
    first = lax.broadcasted_iota(jnp.int32, (8, frame_total), 1) == 0
    out_rows = []
    for g in range(2):
        for a, b in ((0, 0), (0, 1), (1, 1)):
            even = jnp.zeros((8, frame_total), jnp.float32)
            odd = jnp.zeros((8, frame_total), jnp.float32)
            imag = jnp.zeros((8, frame_total), jnp.float32)
            for c in range(2):
                row_a = (c * 4 + g * 2 + a) * 8
                row_b = (c * 4 + g * 2 + b) * 8
                cos_a = spectra[row_a : row_a + 8, :frame_total]
                sin_a = spectra[row_a : row_a + 8, frame_total:]
                cos_b = spectra[row_b : row_b + 8, :frame_total]
                sin_b = spectra[row_b : row_b + 8, frame_total:]
                even += cos_a * cos_b
                odd += sin_a * sin_b
                imag += sin_a * cos_b - cos_a * sin_b
            real = jnp.where(first, even, 2.0 * (even + odd))
            imag = jnp.where(first, odd, 2.0 * imag)
            out_rows.append(jnp.concatenate([real, imag], 1))
    high, low = split(jnp.concatenate(out_rows, 0))
    lags = 2 * out_ref.shape[2]
    both = dot_rows(jnp.concatenate([high, low], 0), table[0, :lags])
    corr = both[:48] + both[48:] + dot_rows(high, table[1, :lags])
    lag = lax.broadcasted_iota(jnp.int32, (1, lags), 1)
    norm = 1.0 / (
        (frame_total - lag).astype(jnp.float32) * jnp.float32(2 * frame_total * 2 * atoms)
    )
    corr = (corr * norm).reshape(6, 8, lags)
    result[0] = corr[:, :, : lags // 2]
    result[1] = corr[:, :, lags // 2 :]
    swap = pltpu.make_async_remote_copy(
        src_ref=result.at[other],
        dst_ref=result_in,
        send_sem=last_send,
        recv_sem=last_recv,
        device_id=(me, other),
        device_id_type=pl.DeviceIdType.MESH,
    )
    swap.start()
    out_ref[:, pl.ds(pl.multiple_of(core * 8, 8), 8), :] = result[core]
    for tg in range(groups):
        pair_copy(tg).wait_send()
        for hop in range(1, tm_size):
            peer_copy(tg, hop).wait_send()
    swap.wait()
    out_ref[:, pl.ds(pl.multiple_of(other * 8, 8), 8), :] = result_in[...]


def per_device_fused(tm_size, positions, velocities, species, wave_vectors):
    frames, atoms = positions.shape[1:]
    waves = wave_vectors.shape[1]
    groups = frames // GROUP
    frame_total = frames * tm_size
    lag_here = frame_total // 4
    vmem = pl.BlockSpec(memory_space=pltpu.VMEM)
    dma = pltpu.SemaphoreType.DMA
    return pl.pallas_call(
        lambda *refs: fused_kernel(tm_size, *refs),
        name="scattering",
        out_shape=jax.ShapeDtypeStruct((6, 16, lag_here), jnp.float32),
        in_specs=[pl.BlockSpec(memory_space=pltpu.HBM)] * 5,
        out_specs=vmem,
        scratch_shapes=[
            pltpu.VMEM(positions.shape, jnp.int32),
            pltpu.VMEM(velocities.shape, jnp.float32),
            pltpu.VMEM((1, atoms), jnp.int32),
            pltpu.VMEM(wave_vectors.shape, jnp.int32),
            pltpu.VMEM((2, frame_total, 2 * frame_total), jnp.bfloat16),
            pltpu.VMEM((3, waves, 128), jnp.float32),
            pltpu.VMEM((waves, 128), jnp.float32),
            pltpu.VMEM((256, atoms), jnp.float32),
            pltpu.VMEM((2 * waves, 256), jnp.float32),
            pltpu.VMEM((groups, 2, tm_size, 8, 128), jnp.float32),
            pltpu.VMEM((groups, tm_size, 8, 128), jnp.float32),
            pltpu.VMEM((groups, tm_size, 8, 128), jnp.float32),
            pltpu.VMEM((tm_size, groups, 8, 128), jnp.float32),
            pltpu.VMEM((2, 6, 8, lag_here), jnp.float32),
            pltpu.VMEM((6, 8, lag_here), jnp.float32),
            dma((5,)),
            dma((groups,)),
            dma((groups,)),
            dma((groups, tm_size)),
            dma((groups, tm_size)),
            dma,
            dma,
        ],
        compiler_params=pltpu.CompilerParams(
            collective_id=0, has_side_effects=True, vmem_limit_bytes=48 << 20
        ),
    )(
        positions,
        velocities,
        species.reshape(1, atoms),
        wave_vectors,
        jnp.asarray(dft_tables(frame_total)),
    )


def solution(mesh):
    tm_size = mesh.shape["tm"]
    atom_size = mesh.shape["atom"]

    def per_device(positions, velocities, species, wave_vectors):
        frames, atoms = positions.shape[1:]
        waves = wave_vectors.shape[1]
        fits = (
            tm_size == 16
            and atom_size == 2
            and frames == 2 * GROUP
            and atoms == 256
            and waves == 256
        )
        if fits:
            return per_device_fused(tm_size, positions, velocities, species, wave_vectors)
        return per_device_general(positions, velocities, species, wave_vectors)

    return jax.shard_map(
        per_device,
        mesh=mesh,
        in_specs=(P(None, "tm", "atom"), P(None, "tm", "atom"), P("atom"), P()),
        out_specs=P(None, "tm", "atom"),
        check_vma=False,
    )
```
